128 devices in a mesh: dp: 16 (over x, y), tensor: 8 (over z, core).
Axes of the slice: x: 4, y: 4, z: 4, core: 2. Of those that a mesh axis runs over, the one named last changes fastest.
Arguments:
- activations: bfloat16 [7168, 8192], P('dp'), may hold values from -6 to 6
- grad_ragged: bfloat16 [7168, 14336], P('dp', 'tensor'), may hold values from -6 to 6
- master: float32 [8192, 7168], P('dp', 'tensor'), may hold values from -0.0625 to 0.0625
- momentum: float32 [8192, 7168], P('dp', 'tensor'), may hold values from -6 to 6
- offsets_full: int32 [16, 9], replicated, may hold values from 0 to 7168, as said below
- offsets_lost: int32 [8], replicated, may hold values from 0 to 7168, as said below
- failed: int32 [1], replicated, may hold values from 0 to 15
Outputs:
- input_grad: bfloat16 [7168, 8192], P('tensor', 'dp')
- new_momentum: float32 [8192, 7168], P('dp', 'tensor')
- new_master: float32 [8192, 7168], P('dp', 'tensor')
- new_weights: bfloat16 [8192, 7168], P(None, 'tensor')
The draws below stay inside these ranges and needn't reach their ends.
Inputs may be any that keep to these rules, and one draw needn't show every extreme that they name: `offsets_full`: each row holds 9 non-falling multiples of 128, the first 0 and the last 7168; no rank owns more than 14 blocks of 128 columns, and in every row some rank owns exactly 14. `offsets_lost`: 8 non-falling multiples of 128, the first 0 and the last 7168, bounds of the first 7 ranks; the last rank owns no column; no rank owns more than 14 blocks of 128 columns, and some rank owns exactly 14.
All inputs are finite; a program needn't handle non-finite values.
Results may differ from the reference program's by a relative error of at most 0.014.
Values may be sent and summed in bfloat16 or wider, within the bound.
No kernel may reach another device: no remote copies, remote signals or barrier semaphores. Data moves between devices by JAX's collectives and lax.ppermute only.
A program may use at most 192 MiB of HBM per device.

```python
import math
import jax
import jax.numpy as jnp
from jax import lax

D = 8192
HID = 7168
TOK = 448
CAP = 1792
CANON = 896
TOKENS = 7168
N_DP = 16
N_TENSOR = 8


def layout_bounds(key, rank_count, block_count, most_blocks):
    key_list = jax.random.split(key, 3)
    rank_ids = jnp.arange(rank_count, dtype=jnp.int32)
    shuffled = jax.random.permutation(key_list[0], rank_count).astype(jnp.int32)
    counts = block_count // rank_count + (shuffled < block_count % rank_count).astype(jnp.int32)
    top_rank = jax.random.randint(key_list[1], (), 0, rank_count).astype(jnp.int32)

    def lift(loop_step, loop_state):
        counts, sub_key = loop_state
        sub_key, pick_key = jax.random.split(sub_key)
        scores = jax.random.randint(pick_key, (rank_count,), 0, 1 << 20) * rank_count + rank_ids
        eligible = (counts > 0) & (rank_ids != top_rank)
        donor_rank = jnp.argmax(jnp.where(eligible, scores, -1))
        needs_more = counts[top_rank] < most_blocks
        moved = (rank_ids == top_rank).astype(jnp.int32) - (rank_ids == donor_rank).astype(jnp.int32)
        return (counts + jnp.where(needs_more, moved, 0), sub_key)
    counts, sub_key = lax.fori_loop(0, most_blocks, lift, (counts, key_list[2]))

    def wander(loop_step, loop_state):
        counts, sub_key = loop_state
        sub_key, pick_give, pick_take = jax.random.split(sub_key, 3)
        give_scores = jax.random.randint(pick_give, (rank_count,), 0, 1 << 20) * rank_count + rank_ids
        take_scores = jax.random.randint(pick_take, (rank_count,), 0, 1 << 20) * rank_count + rank_ids
        can_give = (counts > 0) & (rank_ids != top_rank)
        can_take = (counts < most_blocks) & (rank_ids != top_rank)
        giver_rank = jnp.argmax(jnp.where(can_give, give_scores, -1))
        taker_rank = jnp.argmax(jnp.where(can_take, take_scores, -1))
        movable = jnp.any(can_give) & jnp.any(can_take) & (giver_rank != taker_rank)
        moved = (rank_ids == taker_rank).astype(jnp.int32) - (rank_ids == giver_rank).astype(jnp.int32)
        return (counts + jnp.where(movable, moved, 0), sub_key)
    counts, _ = lax.fori_loop(0, 16 * rank_count, wander, (counts, sub_key))
    return jnp.concatenate([jnp.zeros((1,), jnp.int32), jnp.cumsum(counts).astype(jnp.int32) * 128])


def draw_offsets_full(key, part):
    most_blocks = 2 * HID // (128 * N_TENSOR)
    replica_keys = jax.random.split(jax.random.fold_in(key, 11), N_DP)
    rows = jax.vmap(lambda one_key: layout_bounds(one_key, N_TENSOR, HID // 128, most_blocks))(replica_keys)
    pick_first = jax.random.randint(jax.random.fold_in(key, 31), (), 0, N_DP).astype(jnp.int32)
    pick_step = jax.random.randint(jax.random.fold_in(key, 37), (), 1, N_DP).astype(jnp.int32)
    pick_second = (pick_first + pick_step) % N_DP
    rank_ids = jnp.arange(N_TENSOR, dtype=jnp.int32)
    skew_counts = jnp.where(rank_ids < N_TENSOR // 2, 0, most_blocks).astype(jnp.int32)
    skew_row = jnp.concatenate([jnp.zeros((1,), jnp.int32), jnp.cumsum(skew_counts).astype(jnp.int32) * 128])
    row_ids = jnp.arange(N_DP, dtype=jnp.int32)
    chosen = (row_ids == pick_first) | (row_ids == pick_second)
    return jnp.where(chosen[:, None], skew_row[None, :], rows).astype(jnp.int32)


def draw_offsets_lost(key, part):
    most_blocks = 2 * HID // (128 * N_TENSOR)
    return layout_bounds(jax.random.fold_in(key, 23), N_TENSOR - 1, HID // 128, most_blocks)


def level_of(stream_key, dims, cuts, least, high):
    loudness, own = 1.0, jax.random.fold_in(stream_key, 6)
    for dim, shards_of in cuts:
        draws = jnp.exp(jax.random.uniform(jax.random.fold_in(own, dim), (shards_of,), jnp.float32, least / len(cuts), high / len(cuts)))
        loudness = loudness * jnp.repeat(draws, dims[dim] // shards_of).reshape([-1 if axis == dim else 1 for axis in range(len(dims))])
    return loudness


def bell_draw(rng, extent, spread, limit, shards=(), kind=jnp.bfloat16):
    drawn = jax.random.normal(rng, extent, jnp.float32) * spread
    if len(shards) > 0:
        drawn = level_of(rng, extent, shards, -0.22, 0.18) * drawn
    return jnp.clip(drawn, min=-limit, max=limit).astype(kind)


def setup_inputs(seed: int = 0) -> dict:
    keys = jax.random.split(jax.random.key(seed), 8)
    activations = bell_draw(keys[0], (TOKENS, D), 1.0, 6.0, ((0, 16),))
    grad_ragged = bell_draw(keys[1], (TOKENS, N_TENSOR * CAP), 1.0, 6.0, ((0, 16), (1, 8)))
    master = bell_draw(keys[2], (D, HID), D ** -0.5, 0.0625, ((0, 16), (1, 8)), jnp.float32)
    momentum = bell_draw(keys[3], (D, HID), 1.0, 6.0, ((0, 16), (1, 8)), jnp.float32)
    offsets_full = draw_offsets_full(jax.random.fold_in(keys[7], 71), 0)
    offsets_lost = draw_offsets_lost(jax.random.fold_in(keys[7], 71), 0)
    failed = jax.random.randint(keys[6], (1,), 0, N_DP).astype(jnp.int32)
    return dict(activations=activations, grad_ragged=grad_ragged, master=master, momentum=momentum, offsets_full=offsets_full, offsets_lost=offsets_lost, failed=failed)


def bounds_of(replica, offsets_full, offsets_lost, failed):
    lost_row = jnp.concatenate([offsets_lost, jnp.full((1,), HID, jnp.int32)])
    return jnp.where(failed[0] == replica, lost_row, offsets_full[replica])

def reference(activations, grad_ragged, master, momentum, offsets_full, offsets_lost, failed):
    columns = jnp.arange(HID, dtype=jnp.int32)
    grad_scale = 1.0 / math.sqrt(TOKENS)

    def densify(replica):
        bounds = bounds_of(replica, offsets_full, offsets_lost, failed)
        owner_rank = lax.optimization_barrier(jnp.sum((bounds[None, 1:N_TENSOR] <= columns[:, None]).astype(jnp.int32), axis=1))
        col_index = (owner_rank * CAP + columns - bounds[owner_rank]).astype(jnp.int32)
        rep_rows = lax.dynamic_slice_in_dim(grad_ragged, replica * TOK, TOK, 0)
        return jnp.take(rep_rows, col_index, axis=1)
    dense_grads = lax.map(densify, jnp.arange(N_DP, dtype=jnp.int32))

    def accumulate(running, replica):
        act_rows = lax.dynamic_slice_in_dim(activations, replica * TOK, TOK, 0)
        partial_value = jnp.dot(act_rows.T, dense_grads[replica], preferred_element_type=jnp.float32) * grad_scale
        rounded = lax.optimization_barrier(partial_value.astype(jnp.bfloat16))
        return (running + rounded.astype(jnp.float32), None)
    weight_grad, _ = lax.scan(accumulate, jnp.zeros((D, HID), jnp.float32), jnp.arange(N_DP, dtype=jnp.int32))
    new_momentum = 0.9 * momentum + weight_grad
    new_master = master - 0.01 * new_momentum
    new_weights = new_master.astype(jnp.bfloat16)
    working = master.astype(jnp.bfloat16)
    flat_grads = dense_grads.reshape(TOKENS, HID)

    def add_block(running, col_block):
        grad_cols = lax.dynamic_slice_in_dim(flat_grads, col_block * CANON, CANON, 1)
        weight_cols = lax.dynamic_slice_in_dim(working, col_block * CANON, CANON, 1)
        partial_value = jnp.dot(grad_cols, weight_cols.T, preferred_element_type=jnp.float32)
        rounded = lax.optimization_barrier(partial_value.astype(jnp.bfloat16))
        return (running + rounded.astype(jnp.float32), None)
    input_sum, _ = lax.scan(add_block, jnp.zeros((TOKENS, D), jnp.float32), jnp.arange(N_TENSOR, dtype=jnp.int32))
    return (input_sum.astype(jnp.bfloat16), new_momentum, new_master, new_weights)
```

```python
import functools
import math

import jax
import jax.numpy as jnp
import numpy as np
from jax import lax
from jax.experimental import pallas as pl
from jax.experimental.pallas import tpu as pltpu
from jax.sharding import PartitionSpec as P

SIDE = 4
CORES = 2
LANES = 128
MIB = 1 << 20


def shift_dp(value, dx, dy):
    pairs = [
        (SIDE * x + y, SIDE * ((x + dx) % SIDE) + (y + dy) % SIDE)
        for x in range(SIDE)
        for y in range(SIDE)
    ]
    return lax.ppermute(value, "dp", pairs)


def shift_x(value, step):
    return shift_dp(value, step, 0)


def shift_y(value, step):
    return shift_dp(value, 0, step)


def shift_z(value, step):
    pairs = [
        (CORES * z + c, CORES * ((z + step) % SIDE) + c) for z in range(SIDE) for c in range(CORES)
    ]
    return lax.ppermute(value, "tensor", pairs)


def swap_cores(value):
    pairs = [(CORES * z + c, CORES * z + 1 - c) for z in range(SIDE) for c in range(CORES)]
    return lax.ppermute(value, "tensor", pairs)


def offset_of(z, c, slot):
    dx = CORES * c + slot
    return dx, (dx + z) % SIDE


def send_activations(value, slot):
    ranks = SIDE * CORES
    pairs = []
    for x in range(SIDE):
        for y in range(SIDE):
            for z in range(SIDE):
                for c in range(CORES):
                    dx, dy = offset_of(z, c, slot)
                    there = SIDE * ((x + dx) % SIDE) + (y + dy) % SIDE
                    pairs.append(((SIDE * x + y) * ranks + CORES * z + c, there * ranks + CORES * z + c))
    return lax.ppermute(value, ("dp", "tensor"), pairs)


def scatter_sum_z(own, up, far, down):
    far_a = shift_z(far[0], 1)
    far_b = shift_z(far[1], -1)
    up_b = shift_z(up[1], 1)
    down_a = shift_z(down[0], -1)
    up_a = shift_z(add(up[0], far_a), 1)
    down_b = shift_z(add(down[1], far_b), -1)
    return add(own[0], down_a, up_a), add(own[1], up_b, down_b)


def add(*terms):
    total = terms[0].astype(jnp.float32)
    for term in terms[1:]:
        total = total + term.astype(jnp.float32)
    return total.astype(terms[0].dtype)


def gather_half(value, first, second):
    rows = value.shape[0]
    cut = rows // 2
    one, three = first(value, 1), first(value, -1)
    side_one, side_three = second(value, 1), second(value, -1)
    two = first(one[:cut], 1), first(three[cut:], -1)
    side_two = second(side_one[:cut], 1), second(side_three[cut:], -1)
    line = jnp.concatenate([one, three, *two], axis=0)
    cut = line.shape[0] // 2
    line_one, line_three = second(line, 1), second(line, -1)
    line_two = second(line_one[:cut], 1), second(line_three[cut:], -1)
    early = [value, line, side_one, side_three, *side_two]
    return early, [line_one, line_three], list(line_two)


def gather_plane(half_a, half_b):
    with jax.named_scope("half_a"):
        parts_a = gather_half(half_a, shift_x, shift_y)
    with jax.named_scope("half_b"):
        parts_b = gather_half(half_b, shift_y, shift_x)
    return [a + b for a, b in zip(parts_a, parts_b)]


def _orders():
    turn = (1, 3, 2)
    early, mid, late = [], [], []
    for half in (0, 1):
        def at(along, across):
            return (half, along, across) if half == 0 else (half, across, along)
        early += [at(0, 0)] + [at(k, 0) for k in turn] + [at(0, k) for k in turn]
        mid += [at(k, across) for across in (1, 3) for k in turn]
        late += [at(k, 2) for k in turn]
    return early, mid, late


EARLY, MID, LATE = _orders()
ORDER = EARLY + MID + LATE
PLACE_OF = np.zeros((2, SIDE, SIDE), np.int32)
for _index, _key in enumerate(ORDER):
    PLACE_OF[_key] = _index
PLACE_OF = PLACE_OF.reshape(-1)


def position():
    replica, rank = lax.axis_index("dp"), lax.axis_index("tensor")
    return replica // SIDE, replica % SIDE, rank // CORES, rank % CORES


def run_copies(copies):
    for copy in copies:
        copy.start()
    for copy in copies:
        copy.wait()


def pick_kernel(act_ref, first_ref, second_ref, sems):
    x, y, z, c = position()
    width = first_ref.shape[1]
    copies = []
    for slot, out in enumerate((first_ref, second_ref)):
        dx = CORES * c + slot
        dy = (dx + z) % SIDE
        there = SIDE * ((x + dx) % SIDE) + (y + dy) % SIDE
        columns = pl.ds(pl.multiple_of(there * width, LANES), width)
        copies.append(pltpu.make_async_copy(act_ref.at[:, columns], out, sems.at[slot]))
    run_copies(copies)


def pick(activations, width):
    shape = jax.ShapeDtypeStruct((activations.shape[0], width), activations.dtype)
    size = activations.shape[0] * width * 2
    return pl.pallas_call(
        pick_kernel,
        name="pick",
        out_shape=(shape, shape),
        in_specs=[pl.BlockSpec(memory_space=pl.ANY)],
        out_specs=(pl.BlockSpec(memory_space=pltpu.VMEM),) * 2,
        scratch_shapes=[pltpu.SemaphoreType.DMA((2,))],
        compiler_params=pltpu.CompilerParams(vmem_limit_bytes=4 * MIB),
        cost_estimate=pl.CostEstimate(flops=0, bytes_accessed=4 * size, transcendentals=0),
    )(activations)


def route_kernel(full_ref, lost_ref, failed_ref, own_ref, peer_ref, *outs):
    replica, rank = lax.axis_index("dp"), lax.axis_index("tensor")
    z, c = rank // CORES, rank % CORES
    ranks = SIDE * CORES
    width = outs[0].shape[1]
    half = outs[0].shape[0]
    hidden = width * ranks

    def bound(index):
        kept = full_ref[replica, index]
        lost = jnp.where(index == ranks, hidden, lost_ref[jnp.minimum(index, ranks - 1)])
        return jnp.where(failed_ref[0] == replica, lost, kept) // LANES

    mate = rank + 1 - 2 * c
    low, high = bound(rank), bound(rank + 1)
    mate_low, mate_high = bound(mate), bound(mate + 1)
    for step in range(SIDE):
        target = CORES * ((z + step) % SIDE) + c
        for block in range(width // LANES):
            column = target * (width // LANES) + block
            mine = (column >= low) & (column < high)
            his = (column >= mate_low) & (column < mate_high)
            lanes = slice(block * LANES, (block + 1) * LANES)

            def put(source, start):
                columns = pl.ds(pl.multiple_of((column - start) * LANES, LANES), LANES)
                outs[2 * step][:, lanes] = source[:half, columns]
                outs[2 * step + 1][:, lanes] = source[half:, columns]

            @pl.when(mine)
            def _():
                put(own_ref, low)

            @pl.when(his)
            def _():
                put(peer_ref, mate_low)

            @pl.when(jnp.logical_not(mine | his))
            def _():
                nothing = jnp.zeros((half, LANES), outs[0].dtype)
                outs[2 * step][:, lanes] = nothing
                outs[2 * step + 1][:, lanes] = nothing


def route(own, peer, width, offsets_full, offsets_lost, failed):
    rows = own.shape[0]
    shape = jax.ShapeDtypeStruct((rows // 2, width), own.dtype)
    smem = pl.BlockSpec(memory_space=pltpu.SMEM)
    vmem = pl.BlockSpec(memory_space=pltpu.VMEM)
    outs = pl.pallas_call(
        route_kernel,
        name="route",
        out_shape=(shape,) * (2 * SIDE),
        in_specs=[smem, smem, smem, vmem, vmem],
        out_specs=(vmem,) * (2 * SIDE),
        compiler_params=pltpu.CompilerParams(vmem_limit_bytes=12 * MIB),
        cost_estimate=pl.CostEstimate(
            flops=0, bytes_accessed=rows * width * 16, transcendentals=0
        ),
    )(offsets_full, offsets_lost, failed, own, peer)
    return [(outs[2 * i], outs[2 * i + 1]) for i in range(SIDE)]


def order_kernel(place_ref, *refs):
    pieces, out, sems = refs[:-2], refs[-2], refs[-1]
    _, _, z, c = position()
    rows = out.shape[0] // (2 * SIDE * SIDE)
    copies = []
    for other in range(CORES):
        core = c if other == 0 else 1 - c
        group = pieces[5 * other : 5 * other + 5]
        for shift, sources in ((0, (group[0], group[0])), (3, (group[1], group[1])),
                               (1, (group[2], group[2])), (2, (group[3], group[4]))):
            for slot in range(CORES):
                start = 0 if shift == 2 else slot * 2 * rows
                dx = CORES * core + slot
                dy = (dx + z + shift) % SIDE
                for half in range(2):
                    place = place_ref[half * SIDE * SIDE + dx * SIDE + dy]
                    there = pl.ds(pl.multiple_of(place * rows, 16), rows)
                    copies.append(
                        pltpu.make_async_copy(
                            sources[slot].at[pl.ds(start + half * rows, rows)],
                            out.at[there],
                            sems.at[len(copies)],
                        )
                    )
    run_copies(copies)


def order_activations(pieces):
    width = pieces[0].shape[1]
    rows = pieces[0].shape[0] * SIDE * CORES
    size = rows * width * 2
    return pl.pallas_call(
        order_kernel,
        name="order",
        out_shape=jax.ShapeDtypeStruct((rows, width), pieces[0].dtype),
        in_specs=[pl.BlockSpec(memory_space=pltpu.SMEM)]
        + [pl.BlockSpec(memory_space=pltpu.VMEM)] * len(pieces),
        out_specs=pl.BlockSpec(memory_space=pl.ANY),
        scratch_shapes=[pltpu.SemaphoreType.DMA((2 * SIDE * SIDE,))],
        compiler_params=pltpu.CompilerParams(vmem_limit_bytes=10 * MIB),
        cost_estimate=pl.CostEstimate(flops=0, bytes_accessed=2 * size, transcendentals=0),
    )(jnp.asarray(PLACE_OF), *pieces)


def fold_kernel(*refs):
    groups, out, sems = refs[:-2], refs[-2], refs[-1]
    x, y, z, c = position()
    rows = out.shape[0] // (2 * SIDE * SIDE)
    copies = []
    for group, keys in zip(groups, (EARLY, MID, LATE)):
        for index, (half, dx, dy) in enumerate(keys):
            chip, line = (x - dx + SIDE) % SIDE, (y - dy + SIDE) % SIDE
            away = (line // CORES + c) % CORES
            slot = (chip - z + SIDE) % SIDE
            place = ((away * SIDE + slot) * CORES + line % CORES) * 2 + half
            there = pl.ds(pl.multiple_of(place * rows, 16), rows)
            copies.append(
                pltpu.make_async_copy(
                    group.at[pl.ds(index * rows, rows)], out.at[there], sems.at[len(copies)]
                )
            )
    run_copies(copies)


def fold_inputs(groups):
    width = groups[0].shape[1]
    rows = sum(group.shape[0] for group in groups)
    return pl.pallas_call(
        fold_kernel,
        name="fold",
        out_shape=jax.ShapeDtypeStruct((rows, width), groups[0].dtype),
        in_specs=[pl.BlockSpec(memory_space=pltpu.VMEM)] * len(groups),
        out_specs=pl.BlockSpec(memory_space=pl.ANY),
        scratch_shapes=[pltpu.SemaphoreType.DMA((2 * SIDE * SIDE,))],
        compiler_params=pltpu.CompilerParams(vmem_limit_bytes=10 * MIB),
        cost_estimate=pl.CostEstimate(
            flops=0, bytes_accessed=4 * rows * width, transcendentals=0
        ),
    )(*groups)


def spread_kernel(keys, count, rows, *refs):
    pieces, out, sems = refs[:count], refs[-2], refs[-1]
    x, y, _, _ = position()
    spans = []
    start = 0
    for index, piece in enumerate(pieces):
        spans.append((start, start + piece.shape[0], index))
        start += piece.shape[0]
    copies = []
    for index, (half, dx, dy) in enumerate(keys):
        owner = SIDE * ((x - dx + SIDE) % SIDE) + (y - dy + SIDE) % SIDE
        base = pl.multiple_of((owner * 2 + half) * rows, 16)
        for low, high, which in spans:
            begin, end = max(low, index * rows), min(high, (index + 1) * rows)
            if begin < end:
                there = pl.ds(pl.multiple_of(base + (begin - index * rows), 16), end - begin)
                copies.append(
                    pltpu.make_async_copy(
                        pieces[which].at[pl.ds(begin - low, end - begin)],
                        out.at[there],
                        sems.at[len(copies)],
                    )
                )
    run_copies(copies)


def spread_weights(keys, pieces, rows, whole):
    width = pieces[0].shape[1]
    shape = jax.ShapeDtypeStruct((rows * 2 * SIDE * SIDE, width), pieces[0].dtype)
    operands = list(pieces) + ([] if whole is None else [whole])
    size = sum(piece.size for piece in pieces) * 2
    return pl.pallas_call(
        functools.partial(spread_kernel, keys, len(pieces), rows),
        name="spread",
        out_shape=shape,
        in_specs=[pl.BlockSpec(memory_space=pltpu.VMEM)] * len(pieces)
        + ([] if whole is None else [pl.BlockSpec(memory_space=pl.ANY)]),
        out_specs=pl.BlockSpec(memory_space=pl.ANY),
        input_output_aliases={} if whole is None else {len(pieces): 0},
        scratch_shapes=[pltpu.SemaphoreType.DMA((2 * len(keys),))],
        compiler_params=pltpu.CompilerParams(vmem_limit_bytes=10 * MIB),
        cost_estimate=pl.CostEstimate(flops=0, bytes_accessed=2 * size, transcendentals=0),
    )(*operands)


def local(activations, grad_ragged, master, momentum, offsets_full, offsets_lost, failed):
    tok_rows = activations.shape[0]
    own_rows, canonical = master.shape
    replicas = SIDE * SIDE
    grad_scale = 1.0 / math.sqrt(tok_rows * replicas)

    with jax.named_scope("route"):
        peer = swap_cores(grad_ragged)
        blocks = route(grad_ragged, peer, canonical, offsets_full, offsets_lost, failed)
        grad_a, grad_b = scatter_sum_z(*blocks)

    with jax.named_scope("acts"):
        first, second = pick(activations, own_rows)
        mine = jnp.concatenate(
            [send_activations(first, 0), send_activations(second, 1)], axis=0
        )
        below, above = shift_z(mine, 1), shift_z(mine, -1)
        far = shift_z(below[:tok_rows], 1), shift_z(above[tok_rows:], -1)
        held = [mine, below, above, *far]
        act_rows = order_activations(held + [swap_cores(piece) for piece in held])

    with jax.named_scope("gather_grad"):
        gathered = [jnp.concatenate(parts, axis=0) for parts in gather_plane(grad_a, grad_b)]

    with jax.named_scope("weight"):
        total = None
        start = 0
        for part in gathered:
            term = lax.dot_general(
                act_rows[start : start + part.shape[0]],
                part,
                (((0,), (0,)), ((), ())),
                preferred_element_type=jnp.float32,
            )
            start += part.shape[0]
            total = term if total is None else total + term
        new_momentum = 0.9 * momentum + total * grad_scale
        new_master = master - 0.01 * new_momentum
        shard = new_master.astype(jnp.bfloat16)

    with jax.named_scope("gather_weight"):
        half = own_rows // 2
        pieces = gather_plane(shard[:half], shard[half:])
        new_weights = None
        for keys, parts in zip((EARLY, MID, LATE), pieces):
            new_weights = spread_weights(keys, parts, half, new_weights)

    with jax.named_scope("input"):
        working = master.astype(jnp.bfloat16)
        groups = [
            lax.dot_general(
                part, working, (((1,), (1,)), ((), ())), preferred_element_type=jnp.float32
            ).astype(jnp.bfloat16)
            for part in gathered
        ]
        folded = fold_inputs(groups)
        rows = folded.shape[0] // 2
        paired = add(folded[:rows], swap_cores(folded[rows:]))
        step = rows // SIDE
        blocks = [
            (paired[i * step : i * step + step // 2], paired[i * step + step // 2 : (i + 1) * step])
            for i in range(SIDE)
        ]
        input_grad = jnp.concatenate(scatter_sum_z(*blocks), axis=0)

    return (input_grad, new_momentum, new_master, new_weights)


def solution(mesh):
    placed = (P("dp", None), P("dp", "tensor"), P("dp", "tensor"), P("dp", "tensor"), P(), P(), P())
    return jax.shard_map(
        local,
        mesh=mesh,
        in_specs=placed,
        out_specs=(P("tensor", "dp"), P("dp", "tensor"), P("dp", "tensor"), P(None, "tensor")),
        check_vma=False,
    )
```
